128 devices in a mesh: lon: 64 (over x_hi, z, y, core), lat: 2 (over x_lo).
Axes of the slice: x: 4 (x_hi: 2, x_lo: 2; x = x_hi * 2 + x_lo), y: 4, z: 4, core: 2. Of those that a mesh axis runs over, the one named last changes fastest.
Arguments:
- slab_features: bfloat16 [24, 1024, 1024], P('lat', 'lon'), may hold values from -5 to 5
- upstream_gradient: bfloat16 [24, 1024, 1024], P('lat', 'lon'), may hold values from -4 to 4
- rim_feature_rows: bfloat16 [2, 6, 1024, 1024], P(None, None, 'lon'), may hold values from -5 to 5
- rim_presence_flags: int32 [2, 6], replicated, may hold values 0 or 1
- feature_rescaling_coefficients: float32 [1024], replicated, may hold values from 0.1 to 1.9
- triple_projection_matrix: bfloat16 [1024, 3072], replicated, may hold values from -0.1875 to 0.1875
- final_projection_matrix: bfloat16 [1024, 1024], replicated, may hold values from -0.75 to 0.75
- score_sharpness: float32 [16], replicated, may hold values from 3 to 12
- column_group_decoder_longitude: int32 [24, 256], P('lat', 'lon'), may hold values from 0 to 63, as said below
Outputs:
- decoder_rows: bfloat16 [2, 64, 64, 2, 4, 1024], P('lat', 'lon')
- input_grad: bfloat16 [24, 1024, 1024], P('lat', 'lon')
The draws below stay inside these ranges and needn't reach their ends.
Inputs may be any that keep to these rules, and one draw needn't show every extreme that they name: `column_group_decoder_longitude`: the 48 segments of one device name any one owner at most 2 times; one owner, drawn anew for every draw, is named exactly 2 times by the segments of every device.
All inputs are finite; a program needn't handle non-finite values.
Results may differ from the reference program's by a relative error of at most 0.0085.
Values may be sent and summed in bfloat16 or wider, within the bound.
A program may use at most 128 MiB of HBM per device.

```python
import math
import jax
import jax.numpy as jnp
from jax import lax

D = 1024
ATTN_CHANNELS = 16
HALO = 6
ROWS = 12
COLS = 16
SEG = 4
MOST = 2
NLAT = 24
NLON = 1024
N_LON = 64
N_LAT = 2


def field_draw(key, full_shape):
    key_base, key_cols = jax.random.split(key, 2)
    columns = jnp.exp(jax.random.uniform(key_cols, (full_shape[-1],), jnp.float32, math.log(0.3), math.log(3.0)))
    base_draw = jnp.clip(jax.random.normal(key_base, full_shape, jnp.float32), -3.0, 3.0)
    return 0.5 * columns * base_draw


def draw_slab_features(key, part):
    return field_draw(jax.random.fold_in(key, 11), (NLAT, NLON, D)).astype(jnp.bfloat16)


def draw_rim_feature_rows(key, part):
    return field_draw(jax.random.fold_in(key, 23), (2, HALO, NLON, D)).astype(jnp.bfloat16)


def draw_column_group_decoder_longitude(key, part):
    key_hot, key_blocks = jax.random.split(jax.random.fold_in(key, 37))
    seg_count = COLS // SEG
    block_size = ROWS * seg_count
    hot_owner = jax.random.randint(key_hot, (), 0, N_LON, dtype=jnp.int32)
    owners = jnp.repeat(jnp.arange(N_LON, dtype=jnp.int32), MOST)

    def one_block(block_key):
        key_deck, key_place = jax.random.split(block_key)
        ranking = jax.random.permutation(key_deck, N_LON * MOST).astype(jnp.int32)
        ranking = jnp.where(owners == hot_owner, -1, ranking)
        picked = owners[jnp.argsort(ranking, stable=True)][:block_size]
        return picked[jax.random.permutation(key_place, block_size)]
    labels = jax.vmap(one_block)(jax.random.split(key_blocks, N_LAT * N_LON))
    labels = labels.reshape(N_LAT, N_LON, ROWS, seg_count)
    return labels.transpose(0, 2, 1, 3).reshape(N_LAT * ROWS, N_LON * seg_count)


def set_ends(array, key, least, largest):
    shape = array.shape
    spot = [jax.random.randint(jax.random.fold_in(key, axis), (), 0, shape[axis]) for axis in range(len(shape))]
    array = array.at[tuple(spot)].set(least)
    longest = shape.index(max(shape))
    spot[longest] = (spot[longest] + 1) % shape[longest]
    return array.at[tuple(spot)].set(largest)


def shard_levels(key, dims, shards, low, top_value):
    loudness, own = 1.0, jax.random.fold_in(key, 6)
    for axis_at, parts in shards:
        steps = jnp.exp(jax.random.uniform(jax.random.fold_in(own, axis_at), (parts,), jnp.float32, low / len(shards), top_value / len(shards)))
        loudness = loudness * jnp.repeat(steps, dims[axis_at] // parts).reshape([-1 if axis == axis_at else 1 for axis in range(len(dims))])
    return loudness


def bell_draw(own_key, dims, width, reach, cuts=(), held_as=jnp.bfloat16):
    drawn = jax.random.normal(own_key, dims, jnp.float32) * width
    if len(cuts) > 0:
        drawn = shard_levels(own_key, dims, cuts, -0.22, 0.18) * drawn
    return jnp.clip(drawn, min=-reach, max=reach).astype(held_as)


def setup_inputs(seed: int = 0) -> dict:
    splits = jax.random.split(jax.random.key(seed), 10)
    return {
        "slab_features": draw_slab_features(jax.random.fold_in(splits[9], 71), 0),
        "upstream_gradient": bell_draw(splits[1], (NLAT, NLON, D), 1.0, 4.0, ((0, 2), (1, 64))),
        "rim_feature_rows": draw_rim_feature_rows(jax.random.fold_in(splits[9], 71), 0),
        "rim_presence_flags": set_ends((jax.random.randint(splits[3], (2, HALO), 0, 2) < 1).astype(jnp.int32), jax.random.fold_in(splits[3], 1), 0, 1),
        "feature_rescaling_coefficients": jnp.clip(1.0 + 0.18 * jax.random.normal(splits[4], (D,), jnp.float32), 0.1, 1.9),
        "triple_projection_matrix": bell_draw(splits[5], (D, 3 * D), D ** -0.5, 0.1875),
        "final_projection_matrix": bell_draw(splits[6], (D, D), (D // 16) ** -0.5, 0.75),
        "score_sharpness": jnp.clip(jnp.exp(jax.random.uniform(splits[7], (ATTN_CHANNELS,), jnp.float32, math.log(3.0), math.log(12.0))), 3.0, 12.0),
        "column_group_decoder_longitude": draw_column_group_decoder_longitude(jax.random.fold_in(splits[9], 71), 0),
    }


def rms_normed(vectors, gain_row):
    return vectors * lax.rsqrt(lax.optimization_barrier(jnp.mean(vectors * vectors, axis=-1, keepdims=True)) + 1e-05) * gain_row

def unit_heads(raw_part, channel_count):
    full_shape = raw_part.shape
    per_head = raw_part.reshape(full_shape[:-1] + (channel_count, full_shape[-1] // channel_count))
    per_head = per_head * lax.rsqrt(lax.optimization_barrier(jnp.mean(per_head * per_head, axis=-1, keepdims=True)) + 1e-06)
    return per_head.reshape(full_shape)

def question_multiplier(score_sharpness, feature_dimension):
    channel_count = score_sharpness.shape[0]
    return jnp.repeat(score_sharpness / (feature_dimension // channel_count), feature_dimension // channel_count)

def window_keep(row_count, col_count, halo_width, row_keep):
    ext_rows = row_count + 2 * halo_width
    ext_cols = col_count + 2 * halo_width
    query_ids = jnp.arange(row_count * col_count, dtype=jnp.int32)
    key_ids = jnp.arange(ext_rows * ext_cols, dtype=jnp.int32)
    near_rows = jnp.abs(key_ids[None, :] // ext_cols - halo_width - query_ids[:, None] // col_count) <= halo_width
    near_cols = jnp.abs(key_ids[None, :] % ext_cols - halo_width - query_ids[:, None] % col_count) <= halo_width
    key_keep = jnp.broadcast_to(row_keep[:, None], (ext_rows, ext_cols)).reshape(-1)
    return jnp.where(near_rows & near_cols, key_keep[None, :], 0.0)

def attend(queries, grad_out, ext_kv, keep_mask, channel_count):
    row_count, col_count, feature_dimension = queries.shape
    ext_rows, ext_cols = (ext_kv.shape[0], ext_kv.shape[1])
    head_dim = feature_dimension // channel_count
    query_mat = queries.reshape(row_count * col_count, channel_count, head_dim).astype(jnp.float32)
    flat_kv = ext_kv.reshape(ext_rows * ext_cols, 2 * feature_dimension).astype(jnp.float32)
    key_heads = flat_kv[:, :feature_dimension].reshape(-1, channel_count, head_dim)
    value_heads = flat_kv[:, feature_dimension:].reshape(-1, channel_count, head_dim)
    scores = jnp.einsum('qhd,khd->hqk', query_mat, key_heads)
    weights = jnp.exp(scores) * keep_mask[None]
    attn_probs = weights / lax.optimization_barrier(jnp.sum(weights, axis=-1, keepdims=True))
    probs_low = attn_probs.astype(jnp.bfloat16).astype(jnp.float32)
    mixed_out = jnp.einsum('hqk,khd->qhd', probs_low, value_heads)
    grad_mat = grad_out.reshape(row_count * col_count, channel_count, head_dim).astype(jnp.float32)
    grad_probs = jnp.einsum('qhd,khd->hqk', grad_mat, value_heads)
    inner_sum = lax.optimization_barrier(jnp.sum(attn_probs * grad_probs, axis=-1, keepdims=True))
    grad_scores = (attn_probs * (grad_probs - inner_sum)).astype(jnp.bfloat16).astype(jnp.float32)
    grad_query = jnp.einsum('hqk,khd->qhd', grad_scores, key_heads)
    grad_keys = jnp.einsum('hqk,qhd->khd', grad_scores, query_mat)
    grad_values = jnp.einsum('hqk,qhd->khd', probs_low, grad_mat)
    grad_ext = jnp.concatenate([grad_keys.reshape(ext_rows, ext_cols, feature_dimension), grad_values.reshape(ext_rows, ext_cols, feature_dimension)], axis=-1)
    return (mixed_out.reshape(row_count, col_count, feature_dimension).astype(jnp.bfloat16), grad_query.reshape(row_count, col_count, feature_dimension), grad_ext)

def assemble(blocks):
    feature_dimension = blocks.shape[-1]
    grid = blocks.reshape(N_LAT, N_LON, ROWS, COLS, feature_dimension).transpose(0, 2, 1, 3, 4)
    return grid.reshape(NLAT, NLON, feature_dimension)

def reference(slab_features, upstream_gradient, rim_feature_rows, rim_presence_flags, feature_rescaling_coefficients, triple_projection_matrix, final_projection_matrix, score_sharpness, column_group_decoder_longitude):
    feature_dimension = D
    token_vals = slab_features.astype(jnp.float32)
    normed = rms_normed(token_vals, feature_rescaling_coefficients).astype(jnp.bfloat16)
    projected = jnp.dot(normed, triple_projection_matrix, preferred_element_type=jnp.float32)
    raw_query = projected[..., :feature_dimension]
    raw_keys = projected[..., feature_dimension:2 * feature_dimension]
    multiplier_array = question_multiplier(score_sharpness, feature_dimension)
    query_hat = (unit_heads(raw_query, ATTN_CHANNELS) * multiplier_array).astype(jnp.bfloat16)
    own_kv = jnp.concatenate([unit_heads(raw_keys, ATTN_CHANNELS).astype(jnp.bfloat16), projected[..., 2 * feature_dimension:].astype(jnp.bfloat16)], axis=-1)
    rim_normed = rms_normed(rim_feature_rows.astype(jnp.float32), feature_rescaling_coefficients).astype(jnp.bfloat16)
    rim_proj = jnp.dot(rim_normed, triple_projection_matrix[:, feature_dimension:], preferred_element_type=jnp.float32)
    rim_kv = jnp.concatenate([unit_heads(rim_proj[..., :feature_dimension], ATTN_CHANNELS).astype(jnp.bfloat16), rim_proj[..., feature_dimension:].astype(jnp.bfloat16)], axis=-1)
    full_kv = jnp.concatenate([rim_kv[0], own_kv, rim_kv[1]], axis=0)
    full_kv = jnp.concatenate([full_kv[:, NLON - HALO:], full_kv, full_kv[:, :HALO]], axis=1)
    rim_keep = rim_presence_flags.astype(jnp.float32)
    row_keep = jnp.concatenate([rim_keep[0], jnp.ones((NLAT,), jnp.float32), rim_keep[1]])
    grad_attended = lax.dot_general(upstream_gradient, final_projection_matrix, (((2,), (1,)), ((), ())), preferred_element_type=jnp.float32).astype(jnp.bfloat16)
    ext_rows = ROWS + 2 * HALO
    ext_cols = COLS + 2 * HALO

    def one_block(grad_full, block_index):
        row_start = block_index // N_LON * ROWS
        col_start = block_index % N_LON * COLS
        zero_index = jnp.zeros((), jnp.int32)
        queries = lax.dynamic_slice(query_hat, (row_start, col_start, zero_index), (ROWS, COLS, feature_dimension))
        grad_out = lax.dynamic_slice(grad_attended, (row_start, col_start, zero_index), (ROWS, COLS, feature_dimension))
        ext_kv = lax.dynamic_slice(full_kv, (row_start, col_start, zero_index), (ext_rows, ext_cols, 2 * feature_dimension))
        block_keep = lax.dynamic_slice(row_keep, (row_start,), (ext_rows,))
        mixed_out, grad_query, grad_ext = attend(queries, grad_out, ext_kv, window_keep(ROWS, COLS, HALO, block_keep), ATTN_CHANNELS)
        current = lax.dynamic_slice(grad_full, (row_start, col_start, zero_index), (ext_rows, ext_cols, 2 * feature_dimension))
        grad_full = lax.dynamic_update_slice(grad_full, current + grad_ext, (row_start, col_start, zero_index))
        return (grad_full, (mixed_out, grad_query))
    grad_zero = jnp.zeros(full_kv.shape, jnp.float32)
    grad_full, (mixed_blocks, query_blocks) = lax.scan(one_block, grad_zero, jnp.arange(N_LAT * N_LON, dtype=jnp.int32))
    attended = assemble(mixed_blocks)
    grad_query = assemble(query_blocks)
    output_rows = (token_vals + jnp.dot(attended, final_projection_matrix, preferred_element_type=jnp.float32)).astype(jnp.bfloat16)
    center = grad_full[:, HALO:HALO + NLON]
    center = center + jnp.pad(grad_full[:, NLON + HALO:], ((0, 0), (0, NLON - HALO), (0, 0)))
    center = center + jnp.pad(grad_full[:, :HALO], ((0, 0), (NLON - HALO, 0), (0, 0)))
    grad_kv = center[HALO:HALO + NLAT]
    unused, query_back = jax.vjp(lambda raw_part: unit_heads(raw_part, ATTN_CHANNELS) * multiplier_array, raw_query)
    grad_raw_query = query_back(grad_query)[0]
    unused, key_back = jax.vjp(lambda raw_part: unit_heads(raw_part, ATTN_CHANNELS), raw_keys)
    grad_raw_keys = key_back(grad_kv[..., :feature_dimension])[0]
    grad_projected = jnp.concatenate([grad_raw_query, grad_raw_keys, grad_kv[..., feature_dimension:]], axis=-1).astype(jnp.bfloat16)
    grad_normed = lax.dot_general(grad_projected, triple_projection_matrix, (((2,), (1,)), ((), ())), preferred_element_type=jnp.float32)
    unused, norm_back = jax.vjp(lambda raw_part: rms_normed(raw_part, feature_rescaling_coefficients), token_vals)
    input_grad = (upstream_gradient.astype(jnp.float32) + norm_back(grad_normed)[0]).astype(jnp.bfloat16)
    seg_count = COLS // SEG
    block_size = ROWS * seg_count
    out_blocks = output_rows.reshape(N_LAT, ROWS, N_LON, COLS, D).transpose(0, 2, 1, 3, 4).reshape(N_LAT, N_LON, block_size, SEG * D)
    owner_blocks = column_group_decoder_longitude.reshape(N_LAT, ROWS, N_LON, seg_count).transpose(0, 2, 1, 3).reshape(N_LAT, N_LON, block_size)
    onehot = (owner_blocks[..., None] == jnp.arange(N_LON, dtype=jnp.int32)).astype(jnp.int32)
    earlier = jnp.cumsum(onehot, axis=2) - onehot
    slot_ids = owner_blocks * MOST + lax.optimization_barrier(jnp.sum(earlier * onehot, axis=-1))
    placing = (slot_ids[:, :, None, :] == jnp.arange(N_LON * MOST, dtype=jnp.int32)[:, None]).astype(jnp.float32)
    sent_slots = jnp.einsum('abst,abtw->absw', placing, out_blocks.astype(jnp.float32))
    decoder_rows = sent_slots.reshape(N_LAT, N_LON, N_LON, MOST, SEG, D).transpose(0, 2, 1, 3, 4, 5).astype(jnp.bfloat16)
    return (decoder_rows, input_grad)
```

```python
import functools

import jax
import jax.numpy as jnp
from jax import lax
from jax.experimental import pallas as pl
from jax.experimental.pallas import tpu as pltpu
from jax.sharding import PartitionSpec as P

HEADS = 16
HALO = 6
ROWS = 12
COLS = 16
SEG = 4
EDGE = 8
EXT_ROWS = ROWS + 2 * HALO
EXT_COLS = COLS + 2 * EDGE
TOKENS = ROWS * COLS
KEYS = EXT_ROWS * EXT_COLS
D = 1024
QUAD = 256
QUADS = D // QUAD
PAIR = 128
BLOCK_ROWS = 4
BLOCK_Q = BLOCK_ROWS * COLS
BLOCK_K = (BLOCK_ROWS + 2 * HALO) * EXT_COLS
BLOCKS = ROWS // BLOCK_ROWS
F32 = jnp.float32
BF16 = jnp.bfloat16
MESH = pl.DeviceIdType.MESH


def dot_nn(a, b):
    return lax.dot_general(a, b, (((1,), (0,)), ((), ())), preferred_element_type=F32)


def dot_nt(a, b):
    return lax.dot_general(a, b, (((1,), (1,)), ((), ())), preferred_element_type=F32)


def dot_tn(a, b):
    return lax.dot_general(a, b, (((0,), (0,)), ((), ())), preferred_element_type=F32)


def iota(shape, axis):
    return lax.broadcasted_iota(jnp.int32, shape, axis)


def inverse_rms(x):
    return lax.rsqrt(jnp.mean(x * x, axis=-1, keepdims=True) + 1e-05)


def head_inverse_rms(raw, head_ones):
    return lax.rsqrt(dot_nn((raw * raw).astype(BF16), head_ones) * (1.0 / 64.0) + 1e-06)


def unit_back(raw, grad, head_ones):
    scale = head_inverse_rms(raw, head_ones)
    inner = dot_nn((raw * grad).astype(BF16), head_ones) * (1.0 / 64.0)
    return scale * (grad - raw * (scale * scale * inner))


def layer_kernel(
    lon_count,
    slots,
    x_hbm,
    up_hbm,
    rim_hbm,
    flags,
    gain_hbm,
    w_hbm,
    wo_hbm,
    sharp,
    owners,
    out_hbm,
    grad_hbm,
    x_own,
    up_own,
    gain,
    w,
    wo,
    x_ext,
    n_ext,
    raw_q,
    q_hat,
    grad_att,
    raw_k,
    k_hat,
    v_ones,
    bias,
    head_ones,
    att,
    gk_acc,
    gv_acc,
    gq_acc,
    g_own,
    send_buf,
    recv_left,
    recv_right,
    recv_vert,
    recv_dleft,
    recv_dright,
    out_acc,
    gn_acc,
    slot_buf,
    grad_out,
    local_sem,
    w_sem,
    wo_sem,
    f_send,
    f_recv,
    g_send,
    g_recv,
    a_send,
    a_recv,
):
    lon = lax.axis_index("lon")
    lat = lax.axis_index("lat")
    right = lax.rem(lon + 1, lon_count)
    left = lax.rem(lon + lon_count - 1, lon_count)
    other = 1 - lat

    def to(lat_id, lon_id):
        return {"lat": lat_id, "lon": lon_id}

    def remote(src, dst, send, recv, device):
        return pltpu.make_async_remote_copy(
            src_ref=src,
            dst_ref=dst,
            send_sem=send,
            recv_sem=recv,
            device_id=device,
            device_id_type=MESH,
        )

    vert_src = pl.ds(other * HALO, HALO)
    vert_dst = pl.ds(lat * (ROWS + HALO), HALO)
    rim_dst = pl.ds(lat * (ROWS + HALO), HALO)
    mid = pl.ds(HALO, ROWS)
    first, last = pl.ds(0, EDGE), pl.ds(COLS - EDGE, EDGE)
    e_left, e_own, e_right = pl.ds(0, EDGE), pl.ds(EDGE, COLS), pl.ds(EDGE + COLS, EDGE)
    moves = [
        (x_hbm.at[:, last], x_ext.at[mid, e_left], to(lat, right)),
        (x_hbm.at[:, first], x_ext.at[mid, e_right], to(lat, left)),
        (x_hbm.at[vert_src], x_ext.at[vert_dst, e_own], to(other, lon)),
        (x_hbm.at[vert_src, last], x_ext.at[vert_dst, e_left], to(other, right)),
        (x_hbm.at[vert_src, first], x_ext.at[vert_dst, e_right], to(other, left)),
        (rim_hbm.at[lat, :, last], x_ext.at[rim_dst, e_left], to(lat, right)),
        (rim_hbm.at[lat, :, first], x_ext.at[rim_dst, e_right], to(lat, left)),
    ]
    halo_copies = [
        remote(src, dst, f_send.at[i], f_recv.at[i], dev) for i, (src, dst, dev) in enumerate(moves)
    ]
    local_copies = [
        pltpu.make_async_copy(x_hbm, x_own, local_sem.at[0]),
        pltpu.make_async_copy(gain_hbm, gain, local_sem.at[1]),
        pltpu.make_async_copy(up_hbm, up_own, local_sem.at[2]),
        pltpu.make_async_copy(x_hbm, x_ext.at[mid, e_own], local_sem.at[3]),
        pltpu.make_async_copy(rim_hbm.at[lat], x_ext.at[rim_dst, e_own], local_sem.at[4]),
    ]
    w_copies = [
        [
            pltpu.make_async_copy(
                w_hbm.at[:, pl.ds(part * D + j * QUAD, QUAD)], w.at[part, j], w_sem.at[part, j]
            )
            for j in range(QUADS)
        ]
        for part in range(3)
    ]
    wo_copy = pltpu.make_async_copy(wo_hbm, wo, wo_sem.at[0])
    for copy in halo_copies:
        copy.start()
    for copy in local_copies:
        copy.start()
    for copy in w_copies[0]:
        copy.start()
    wo_copy.start()
    for j in range(QUADS):
        w_copies[1][j].start()
        w_copies[2][j].start()

    lane_head = iota((QUAD, QUAD), 1) // 64
    head_ones[...] = jnp.where(iota((QUAD, QUAD), 0) // 64 == lane_head, 1.0, 0.0).astype(BF16)
    for p in range(2):
        v_ones[p, :, PAIR:] = jnp.ones((KEYS, PAIR), BF16)
    key_row = iota((1, BLOCK_K), 1) // EXT_COLS
    near = (
        jnp.abs(
            iota((BLOCK_Q, BLOCK_K), 1) // EXT_COLS - HALO - iota((BLOCK_Q, BLOCK_K), 0) // COLS
        )
        <= HALO
    ) & (
        jnp.abs(iota((BLOCK_Q, BLOCK_K), 1) % EXT_COLS - EDGE - iota((BLOCK_Q, BLOCK_K), 0) % COLS)
        <= HALO
    )
    for i in range(BLOCKS):
        keep = jnp.ones((1, BLOCK_K), F32)
        for r in range(HALO):
            flag = flags[lat, r].astype(F32)
            keep = jnp.where(
                key_row + BLOCK_ROWS * i == lat * (ROWS + HALO) + r,
                jnp.broadcast_to(flag, (1, BLOCK_K)),
                keep,
            )
        bias[i] = jnp.where(near & (keep > 0.5), 0.0, -1e30)

    local_copies[0].wait()
    local_copies[1].wait()
    local_copies[2].wait()
    gains = gain[...]
    own = x_own[...].reshape(TOKENS, D).astype(F32)
    n_own = (own * inverse_rms(own) * gains).astype(BF16)
    up_rows = up_own[...].reshape(TOKENS, D)
    ones = head_ones[...]
    lane_of_quad = iota((1, QUAD), 1) // 64
    wo_copy.wait()
    for j in range(QUADS):
        w_copies[0][j].wait()
        raw = dot_nn(n_own, w[0, j])
        raw_q[j] = raw
        scale = jnp.zeros((1, QUAD), F32)
        for h in range(4):
            scale = jnp.where(
                lane_of_quad == h,
                jnp.broadcast_to(sharp[j * 4 + h] * (1.0 / 64.0), (1, QUAD)),
                scale,
            )
        q_hat[j] = (raw * head_inverse_rms(raw, ones) * scale).astype(BF16)
        grad_att[j] = dot_nt(up_rows, wo[j]).astype(BF16)

    local_copies[3].wait()
    local_copies[4].wait()
    for copy in halo_copies:
        copy.wait()
    ext = x_ext[...].reshape(KEYS, D).astype(F32)
    n_ext[...] = (ext * inverse_rms(ext) * gains).astype(BF16)
    for j in range(QUADS):
        w_copies[1][j].wait()
        w_copies[2][j].wait()
    out_acc[...] = own
    gn_acc[...] = jnp.zeros((TOKENS, D), F32)

    def grad_copies(j):
        rows_out = pl.ds(other * (ROWS + HALO), HALO)
        buf = send_buf.at[j]
        plans = [
            (buf.at[:, mid, e_right], recv_left.at[j], to(lat, right)),
            (buf.at[:, mid, e_left], recv_right.at[j], to(lat, left)),
            (buf.at[:, rows_out, e_own], recv_vert.at[j], to(other, lon)),
            (buf.at[:, rows_out, e_right], recv_dleft.at[j], to(other, right)),
            (buf.at[:, rows_out, e_left], recv_dright.at[j], to(other, left)),
        ]
        return [
            remote(src, dst, g_send.at[j, i], g_recv.at[j, i], dev)
            for i, (src, dst, dev) in enumerate(plans)
        ]

    low = iota((BLOCK_Q, PAIR), 1) < 64
    none = jnp.zeros((BLOCK_Q, PAIR), BF16)

    def by_head(rows):
        return jnp.concatenate([jnp.where(low, rows, none), jnp.where(low, none, rows)], axis=0)

    def own_head(rows):
        return jnp.where(low, rows[:BLOCK_Q], rows[BLOCK_Q:])

    def one_quad(j, carry):
        keys = dot_nn(n_ext[...], w[1, j])
        k_hat[...] = (keys * head_inverse_rms(keys, ones)).astype(BF16)
        raw_k[j] = keys.reshape(EXT_ROWS, EXT_COLS, QUAD)[
            HALO : HALO + ROWS, EDGE : EDGE + COLS
        ].reshape(TOKENS, QUAD)
        values = dot_nn(n_ext[...], w[2, j]).astype(BF16)
        for p in range(2):
            v_ones[p, :, :PAIR] = values[:, p * PAIR : (p + 1) * PAIR]
        gk_acc[...] = jnp.zeros((KEYS, QUAD), F32)
        gv_acc[...] = jnp.zeros((KEYS, QUAD), F32)
        for p in range(2):
            lanes = slice(p * PAIR, (p + 1) * PAIR)
            for i in range(BLOCKS):
                rows = slice(i * BLOCK_Q, (i + 1) * BLOCK_Q)
                cells = slice(i * BLOCK_ROWS * EXT_COLS, i * BLOCK_ROWS * EXT_COLS + BLOCK_K)
                queries = by_head(q_hat[j, rows, lanes])
                pair_keys = k_hat[cells, lanes]
                scores = dot_nt(queries, pair_keys)
                block_bias = bias[i]
                weights = jnp.exp(scores + jnp.concatenate([block_bias, block_bias], axis=0))
                weights_low = weights.astype(BF16)
                mixed = dot_nn(weights_low, v_ones[p, cells, :])
                inverse = 1.0 / own_head(mixed[:, PAIR:])
                attended = own_head(mixed[:, :PAIR]) * inverse
                att[rows, lanes] = attended.astype(BF16)
                grads = (grad_att[j, rows, lanes].astype(F32) * inverse).astype(BF16)
                inner = (-(grads.astype(F32) * attended)).astype(BF16)
                pair_grads = by_head(grads)
                grad_side = jnp.concatenate([pair_grads, by_head(inner)], axis=1)
                grad_scores = (weights * dot_nt(grad_side, v_ones[p, cells, :])).astype(BF16)
                gq_acc[rows, lanes] = own_head(dot_nn(grad_scores, pair_keys))
                gk_acc[cells, lanes] += dot_tn(grad_scores, queries)
                gv_acc[cells, lanes] += dot_tn(weights_low, pair_grads)
        for part, acc in ((0, gk_acc), (1, gv_acc)):
            grid = acc[...].reshape(EXT_ROWS, EXT_COLS, QUAD)
            send_buf[j, part] = grid.astype(BF16)
            g_own[j, part] = grid[HALO : HALO + ROWS, EDGE : EDGE + COLS]
        for copy in grad_copies(j):
            copy.start()
        out_acc[...] += dot_nn(att[...], wo[j])
        scale = jnp.zeros((1, QUAD), F32)
        for h in range(4):
            scale = jnp.where(
                lane_of_quad == h,
                jnp.broadcast_to(sharp[j * 4 + h] * (1.0 / 64.0), (1, QUAD)),
                scale,
            )
        grad_raw = unit_back(raw_q[j], gq_acc[...] * scale, ones)
        gn_acc[...] += dot_nt(grad_raw.astype(BF16), w[0, j])
        return carry

    lax.fori_loop(0, QUADS, one_quad, 0)

    segments = TOKENS // SEG
    per_row = COLS // SEG
    lane_seg = iota((1, TOKENS), 1) // SEG
    owner = jnp.zeros((1, TOKENS), jnp.int32)
    for s in range(segments):
        owner = jnp.where(
            lane_seg == s,
            jnp.broadcast_to(owners[s // per_row, s % per_row], (1, TOKENS)),
            owner,
        )
    earlier = jnp.zeros((1, TOKENS), jnp.int32)
    for s in range(segments):
        same = owner == jnp.broadcast_to(owners[s // per_row, s % per_row], (1, TOKENS))
        earlier += jnp.where(same & (lane_seg > s), 1, 0)
    place = (owner * slots + earlier) * SEG + iota((1, TOKENS), 1) % SEG
    slot_rows = lon_count * slots * SEG
    placing = jnp.where(
        iota((slot_rows, TOKENS), 0) == jnp.broadcast_to(place, (slot_rows, TOKENS)), 1.0, 0.0
    ).astype(BF16)
    output_rows = out_acc[...].astype(BF16)
    slot_buf[...] = dot_nn(placing, output_rows).astype(BF16).reshape(lon_count, slots * SEG, D)

    def handoff(k):
        target = lax.rem(lon + k, lon_count)
        return remote(
            slot_buf.at[target], out_hbm.at[lon], a_send.at[0], a_recv.at[0], to(lat, target)
        )

    @pl.loop(1, lon_count)
    def _(k):
        handoff(k).start()

    keep_own = pltpu.make_async_copy(slot_buf.at[lon], out_hbm.at[lon], local_sem.at[0])
    keep_own.start()

    vert_add = pl.ds(other * HALO, HALO)

    def one_tail(j, carry):
        for copy in grad_copies(j):
            copy.wait()
        g_own[j, :, :, 0:EDGE] += recv_left[j].astype(F32)
        g_own[j, :, :, COLS - EDGE : COLS] += recv_right[j].astype(F32)
        g_own[j, :, vert_add] += recv_vert[j].astype(F32)
        g_own[j, :, vert_add, 0:EDGE] += recv_dleft[j].astype(F32)
        g_own[j, :, vert_add, COLS - EDGE : COLS] += recv_dright[j].astype(F32)
        grad_raw = unit_back(raw_k[j], g_own[j, 0].reshape(TOKENS, QUAD), ones)
        gn_acc[...] += dot_nt(grad_raw.astype(BF16), w[1, j]) + dot_nt(
            g_own[j, 1].reshape(TOKENS, QUAD).astype(BF16), w[2, j]
        )
        return carry

    lax.fori_loop(0, QUADS, one_tail, 0)
    tokens = x_own[...].reshape(TOKENS, D).astype(F32)
    scale = inverse_rms(tokens)
    scaled = gn_acc[...] * gains
    inner = jnp.mean(tokens * scaled, axis=-1, keepdims=True)
    total = up_own[...].reshape(TOKENS, D).astype(F32) + scale * (
        scaled - tokens * (scale * scale * inner)
    )
    grad_out[...] = total.astype(BF16).reshape(ROWS, COLS, D)
    write_back = pltpu.make_async_copy(grad_out, grad_hbm, local_sem.at[1])
    write_back.start()
    write_back.wait()
    keep_own.wait()
    most = pl.ds(0, lon_count - 1)
    everyone = remote(slot_buf.at[most], out_hbm.at[most], a_send.at[0], a_recv.at[0], to(lat, right))
    everyone.wait()


def per_device(
    slab_features,
    upstream_gradient,
    rim_feature_rows,
    rim_presence_flags,
    feature_rescaling_coefficients,
    triple_projection_matrix,
    final_projection_matrix,
    score_sharpness,
    column_group_decoder_longitude,
):
    lon_count = lax.axis_size("lon")
    segments = TOKENS // SEG
    slots = max(2, (2 * segments + lon_count - 1) // lon_count)
    hbm = pl.BlockSpec(memory_space=pl.ANY)
    smem = pl.BlockSpec(memory_space=pltpu.SMEM)
    dma = pltpu.SemaphoreType.DMA
    decoder_rows, input_grad = pl.pallas_call(
        functools.partial(layer_kernel, lon_count, slots),
        out_shape=(
            jax.ShapeDtypeStruct((lon_count, slots * SEG, D), BF16),
            jax.ShapeDtypeStruct((ROWS, COLS, D), BF16),
        ),
        in_specs=[hbm, hbm, hbm, smem, hbm, hbm, hbm, smem, smem],
        out_specs=(hbm, hbm),
        scratch_shapes=[
            pltpu.VMEM((ROWS, COLS, D), BF16),
            pltpu.VMEM((ROWS, COLS, D), BF16),
            pltpu.VMEM((1, D), F32),
            pltpu.VMEM((3, QUADS, D, QUAD), BF16),
            pltpu.VMEM((QUADS, QUAD, D), BF16),
            pltpu.VMEM((EXT_ROWS, EXT_COLS, D), BF16),
            pltpu.VMEM((KEYS, D), BF16),
            pltpu.VMEM((QUADS, TOKENS, QUAD), F32),
            pltpu.VMEM((QUADS, TOKENS, QUAD), BF16),
            pltpu.VMEM((QUADS, TOKENS, QUAD), BF16),
            pltpu.VMEM((QUADS, TOKENS, QUAD), F32),
            pltpu.VMEM((KEYS, QUAD), BF16),
            pltpu.VMEM((2, KEYS, 2 * PAIR), BF16),
            pltpu.VMEM((BLOCKS, BLOCK_Q, BLOCK_K), F32),
            pltpu.VMEM((QUAD, QUAD), BF16),
            pltpu.VMEM((TOKENS, QUAD), BF16),
            pltpu.VMEM((KEYS, QUAD), F32),
            pltpu.VMEM((KEYS, QUAD), F32),
            pltpu.VMEM((TOKENS, QUAD), F32),
            pltpu.VMEM((QUADS, 2, ROWS, COLS, QUAD), F32),
            pltpu.VMEM((QUADS, 2, EXT_ROWS, EXT_COLS, QUAD), BF16),
            pltpu.VMEM((QUADS, 2, ROWS, EDGE, QUAD), BF16),
            pltpu.VMEM((QUADS, 2, ROWS, EDGE, QUAD), BF16),
            pltpu.VMEM((QUADS, 2, HALO, COLS, QUAD), BF16),
            pltpu.VMEM((QUADS, 2, HALO, EDGE, QUAD), BF16),
            pltpu.VMEM((QUADS, 2, HALO, EDGE, QUAD), BF16),
            pltpu.VMEM((TOKENS, D), F32),
            pltpu.VMEM((TOKENS, D), F32),
            pltpu.VMEM((lon_count, slots * SEG, D), BF16),
            pltpu.VMEM((ROWS, COLS, D), BF16),
            dma((5,)),
            dma((3, QUADS)),
            dma((1,)),
            dma((7,)),
            dma((7,)),
            dma((QUADS, 5)),
            dma((QUADS, 5)),
            dma((1,)),
            dma((1,)),
        ],
        compiler_params=pltpu.CompilerParams(
            has_side_effects=True, vmem_limit_bytes=56 * 1024 * 1024
        ),
        name="layer",
    )(
        slab_features,
        upstream_gradient,
        rim_feature_rows,
        rim_presence_flags,
        feature_rescaling_coefficients.reshape(1, D),
        triple_projection_matrix,
        final_projection_matrix.reshape(QUADS, QUAD, D),
        score_sharpness,
        column_group_decoder_longitude,
    )
    return (decoder_rows.reshape(1, 1, lon_count, slots, SEG, D), input_grad)


def solution(mesh):
    return jax.shard_map(
        per_device,
        mesh=mesh,
        in_specs=(
            P("lat", "lon", None),
            P("lat", "lon", None),
            P(None, None, "lon", None),
            P(),
            P(),
            P(),
            P(),
            P(),
            P("lat", "lon"),
        ),
        out_specs=(P("lat", "lon", None, None, None, None), P("lat", "lon", None)),
        check_vma=False,
    )
```
